1024 devices in a mesh: ctx: 64 (over z, x), ch: 16 (over y, core).
Axes of the slice: x: 8, y: 8, z: 8, core: 2. Of those that a mesh axis runs over, the one named last changes fastest.
Arguments:
- signal: bfloat16 [16384, 4096], P('ctx', 'ch'), may hold values from -6 to 6
- upstream: bfloat16 [16384, 8192], P('ctx', 'ch'), may hold values from -6 to 6
- out_weight: bfloat16 [4096, 8192], P(None, 'ch'), may hold values from -0.0625 to 0.0625
- residues: float32 [4096, 16], P('ch'), may hold values from -6 to 6
- decays: float32 [4096, 16], P('ch'), may hold values from 0.5 to 300
- skip_gain: float32 [4096], P('ch'), may hold values from 0.2 to 1
Outputs:
- grad_signal: bfloat16 [16384, 4096], P('ctx', 'ch')
- grad_residues: float32 [4096, 16], P('ch')
- grad_decays: float32 [4096, 16], P('ch')
- grad_skip: float32 [4096], P('ch')
The draws below stay inside these ranges and needn't reach their ends.
All inputs are finite; a program needn't handle non-finite values.
Results may differ from the reference program's by a relative error of at most 0.019.
Values may be sent and summed in bfloat16 or wider, within the bound.
A program may use at most 32 MiB of HBM per device.

```python
import math
import jax
import jax.numpy as jnp
from jax import lax

D = 4096
DOUT = 8192
ORDER = 16
SEQ = 16384
N_CH = 16


def levels(stream_key, shape, split, low, top_value):
    gain = 1.0
    for dim, blocks in split:
        heights = jax.random.uniform(jax.random.fold_in(jax.random.fold_in(stream_key, 6), dim), (blocks,), jnp.float32, low / len(split), top_value / len(split))
        gain = gain * jnp.repeat(jnp.exp(heights), shape[dim] // blocks).reshape((-1,) + (1,) * (len(shape) - 1 - dim))
    return gain


def normal_values(rng, shape, deviation, reach, cuts=(), held_as=jnp.bfloat16):
    gain = levels(rng, shape, cuts, -0.22, 0.18) if cuts else 1.0
    drawn = jax.random.normal(rng, shape, jnp.float32) * deviation * gain
    return jnp.minimum(jnp.maximum(drawn, -reach), reach).astype(held_as)


def setup_inputs(seed: int = 0) -> dict:
    streams_of = jax.random.split(jax.random.key(seed), 7)
    return {
        "signal": normal_values(streams_of[0], (SEQ, D), 1.0, 6.0, ((0, 64), (1, 16))),
        "upstream": normal_values(streams_of[1], (SEQ, DOUT), 1.0, 6.0, ((0, 64), (1, 16))),
        "out_weight": normal_values(streams_of[2], (D, DOUT), DOUT ** -0.5, 0.0625, ((1, 16),)),
        "residues": normal_values(streams_of[3], (D, ORDER), 1.0, 6.0, ((0, 16),), jnp.float32),
        "decays": jnp.clip(jnp.exp(math.log(300.0) - 6.3969297 * jax.random.uniform(streams_of[4], (D, ORDER), jnp.float32) ** levels(streams_of[4], (D, ORDER), ((0, 16),), -0.2, 0.2)), 0.5, 300.0),
        "skip_gain": jnp.clip(0.2 + 0.8 * jax.random.uniform(streams_of[5], (D,), jnp.float32) ** levels(streams_of[5], (D,), ((0, 16),), -0.2, 0.2), 0.2, 1.0),
    }


def reference(signal, upstream, out_weight, residues, decays, skip_gain):
    block = DOUT // N_CH
    total = jnp.zeros((SEQ, D), jnp.float32)
    for index in range(N_CH):
        part = jnp.dot(upstream[:, index * block:(index + 1) * block], out_weight[:, index * block:(index + 1) * block].T, preferred_element_type=jnp.float32)
        part = lax.optimization_barrier(part.astype(jnp.bfloat16))
        total = total + part.astype(jnp.float32)
    grad_conv = total.astype(jnp.bfloat16).astype(jnp.float32)
    sig = signal.astype(jnp.float32)
    padded = 2 * SEQ
    frac = jnp.arange(SEQ, dtype=jnp.float32) / SEQ
    filt = jnp.zeros((SEQ, D), jnp.float32)
    for mode in range(ORDER):
        filt = filt + residues[:, mode][None, :] * jnp.exp(-decays[:, mode][None, :] * frac[:, None])
    filt = filt / jnp.sqrt(jnp.float32(SEQ))
    spec_conv = jnp.fft.rfft(grad_conv, n=padded, axis=0)
    spec_sig = jnp.fft.rfft(sig, n=padded, axis=0)
    spec_filt = jnp.fft.rfft(filt, n=padded, axis=0)
    conv_back = jnp.fft.irfft(jnp.conj(spec_filt) * spec_conv, n=padded, axis=0)[:SEQ]
    grad_signal = (conv_back + skip_gain[None, :] * grad_conv).astype(jnp.bfloat16)
    grad_filt = jnp.fft.irfft(jnp.conj(spec_sig) * spec_conv, n=padded, axis=0)[:SEQ]
    res_cols = []
    dec_cols = []
    for mode in range(ORDER):
        power = jnp.exp(-decays[:, mode][None, :] * frac[:, None])
        res_cols.append(lax.optimization_barrier(jnp.sum(grad_filt * power, axis=0)) / SEQ)
        dec_cols.append(-residues[:, mode] * lax.optimization_barrier(jnp.sum(grad_filt * power * frac[:, None], axis=0)) / SEQ)
    grad_residues = jnp.stack(res_cols, axis=1).astype(jnp.float32)
    grad_decays = jnp.stack(dec_cols, axis=1).astype(jnp.float32)
    grad_skip = (lax.optimization_barrier(jnp.sum(grad_conv * sig, axis=0)) / jnp.sqrt(jnp.float32(SEQ))).astype(jnp.float32)
    return (grad_signal, grad_residues, grad_decays, grad_skip)
```

```python
import functools

import jax
import jax.numpy as jnp
from jax import lax
from jax.experimental import pallas as pl
from jax.experimental.pallas import tpu as pltpu
from jax.sharding import PartitionSpec as P

MESH = pl.DeviceIdType.MESH
F32 = jnp.float32
BF16 = jnp.bfloat16
RING = 8
PLUS_BLOCKS = (0, 1, 1, 3, 3, 5, 5)
MINUS_BLOCKS = (0, 2, 2, 4, 4, 6, 6)
SLOTS = len(PLUS_BLOCKS)


def kernel(
    sig_h, up_h, w_h, res_h, dec_h, skip_h,
    out, res_o, dec_o, skip_o,
    sig_v, up_v, w_v, res_v, dec_v, skip_v,
    sig_f, pair_s, pair_r, own, ring_s, ring_r, gc, yl,
    tile, rows_x, rows_z, local_in, back, full, state_in,
    local_sem, w_sem, pair_ss, pair_rs, ring_ss, ring_rs, x_ss, x_rs, z_ss, z_rs, b_ss, b_rs,
):
    tokens, width = sig_h.shape
    half_rows = tokens // 2
    lanes = width // 2
    modes = res_h.shape[0]
    length = tokens * RING * RING
    ctx = lax.axis_index("ctx")
    ch = lax.axis_index("ch")
    z, x = lax.div(ctx, RING), lax.rem(ctx, RING)
    y, core = lax.div(ch, 2), lax.rem(ch, 2)

    def at_x(step):
        return (z * RING + lax.rem(x + step, RING), ch)

    def at_z(step):
        return (lax.rem(z + step, RING) * RING + x, ch)

    def at_y(step):
        return (ctx, lax.rem(y + step, RING) * 2 + core)

    partner = (ctx, y * 2 + 1 - core)

    barrier = pltpu.get_barrier_semaphore()
    peers = [partner, at_y(1), at_y(RING - 1)]
    peers += [at_x(step) for step in range(1, RING)] + [at_z(step) for step in range(1, RING)]
    for peer in peers:
        pl.semaphore_signal(barrier, inc=1, device_id=peer, device_id_type=MESH)

    def w_copy(index):
        offset = lax.div(index + 1, 2)
        dest = lax.rem(y + 4 + (2 * lax.rem(index, 2) - 1) * -offset + RING, RING)
        return pltpu.make_async_copy(
            w_h.at[pl.ds(dest * 2 * width, 2 * width), :], w_v.at[index], w_sem.at[index]
        )

    loads = [
        pltpu.make_async_copy(src, dst, local_sem.at[n])
        for n, (src, dst) in enumerate(
            ((up_h, up_v), (dec_h, dec_v), (res_h, res_v), (skip_h, skip_v), (sig_h, sig_v))
        )
    ]
    loads[0].start()
    w_copy(jnp.int32(0)).start()
    w_copy(jnp.int32(1)).start()
    for load in loads[1:]:
        load.start()
    for index in range(2, RING):
        w_copy(jnp.int32(index)).start()

    loads[0].wait()

    def product(index, carry):
        w_copy(index).wait()
        theirs = w_v[index, pl.ds(pl.multiple_of((1 - core) * width, width), width), :]
        pair_s[index] = lax.dot_general(
            up_v[...], theirs, (((1,), (1,)), ((), ())), preferred_element_type=F32
        ).astype(BF16)
        mine = w_v[index, pl.ds(pl.multiple_of(core * width, width), width), :]
        own[index] = lax.dot_general(
            up_v[...], mine, (((1,), (1,)), ((), ())), preferred_element_type=F32
        )
        return carry

    lax.fori_loop(0, RING, product, 0)
    pl.semaphore_wait(barrier, len(peers))

    def pair_copy(index):
        return pltpu.make_async_remote_copy(
            src_ref=pair_s.at[index], dst_ref=pair_r.at[index],
            send_sem=pair_ss.at[index], recv_sem=pair_rs.at[index],
            device_id=partner, device_id_type=MESH,
        )

    def ring_copy(way, slot):
        return pltpu.make_async_remote_copy(
            src_ref=ring_s.at[way, slot], dst_ref=ring_r.at[way, slot],
            send_sem=ring_ss.at[way, slot], recv_sem=ring_rs.at[way, slot],
            device_id=at_y(1 if way == 0 else RING - 1), device_id_type=MESH,
        )

    for index in range(RING):
        pair_copy(index).start()
    arrived = set()

    def chip_sum(index, half):
        if index not in arrived:
            arrived.add(index)
            pair_copy(index).wait_recv()
        span = pl.ds(half * half_rows, half_rows)
        return own[index, span, :] + pair_r[index, span, :].astype(F32)

    def ring_step(slot):
        for way, blocks in enumerate((PLUS_BLOCKS, MINUS_BLOCKS)):
            total = chip_sum(blocks[slot], (slot + way) % 2)
            if slot >= 2:
                ring_copy(way, slot - 2).wait_recv()
                total = total + ring_r[way, slot - 2].astype(F32)
            ring_s[way, slot] = total.astype(BF16)
            ring_copy(way, slot).start()

    ring_step(0)
    ring_step(1)

    for load in loads[1:]:
        load.wait()
    pole = jnp.exp(dec_v[...] * (-1.0 / length))
    pole_block = jnp.exp(dec_v[...] * (-float(tokens) / length))
    gain = res_v[...] * (1.0 / length**0.5)
    sig_f[...] = sig_v[...].astype(F32)
    zero = jnp.zeros((modes, width), F32)

    def signal_steps(group, carry):
        state, slope = carry
        for step in range(8):
            row = sig_f[pl.ds(group * 8 + step, 1), :]
            state = (state + row) * pole
            slope = slope * pole + state
        return state, slope

    sig_state, sig_slope = lax.fori_loop(0, tokens // 8, signal_steps, (zero, zero))

    for slot in range(2, SLOTS):
        ring_step(slot)
    for half in (1, 0):
        total = chip_sum(RING - 1, half)
        for way in (0, 1):
            slot = SLOTS - 1 - (half + way) % 2
            ring_copy(way, slot).wait_recv()
            total = total + ring_r[way, slot].astype(F32)
        gc[pl.ds(half * half_rows, half_rows), :] = total.astype(BF16).astype(F32)

    skip_sum = jnp.sum(gc[...] * sig_f[...], axis=0, keepdims=True)

    def gradient_steps(group, carry):
        state, slope, res_sum, dec_sum = carry
        for step in range(8):
            pos = tokens - 1 - (group * 8 + step)
            grad = gc[pl.ds(pos, 1), :]
            row = sig_f[pl.ds(pos, 1), :]
            moved = state * pole
            state = grad + moved
            slope = slope * pole + moved
            res_sum = res_sum + row * state
            dec_sum = dec_sum + row * slope
            yl[pl.ds(pos, 1), :] = jnp.sum(gain * state, axis=0, keepdims=True)
        return state, slope, res_sum, dec_sum

    state, slope, res_sum, dec_sum = lax.fori_loop(
        0, tokens // 8, gradient_steps, (zero, zero, zero, zero)
    )

    parts = (
        state, slope, sig_state, sig_slope, res_sum, dec_sum,
        jnp.broadcast_to(skip_sum, (modes, width)), pole_block,
    )
    for line, part in enumerate(parts):
        for half in (0, 1):
            for first in range(0, modes, 8):
                tile[pl.ds((half * modes + first) * 8 + line, 8, stride=8), :] = part[
                    first : first + 8, half * lanes : (half + 1) * lanes
                ]
    share = 2 * modes // RING
    span = share * 8

    def x_copy(step):
        peer = lax.rem(x + step, RING)
        return pltpu.make_async_remote_copy(
            src_ref=tile.at[pl.ds(pl.multiple_of(peer * span, 8), span), :], dst_ref=rows_x.at[x],
            send_sem=x_ss.at[step], recv_sem=x_rs.at[step],
            device_id=at_x(step), device_id_type=MESH,
        )

    for step in range(1, RING):
        x_copy(step).start()
    rows_x[x] = tile[pl.ds(pl.multiple_of(x * span, 8), span), :]
    for step in range(1, RING):
        x_copy(step).wait_recv()

    def line_of(ref, index, line):
        return ref[index, pl.ds(line, share, stride=8), :]

    empty = jnp.zeros((share, lanes), F32)
    jump = line_of(rows_x, 0, 7)
    state, slope, res_sum, dec_sum, skip_sum = empty, empty, empty, empty, empty
    for block in reversed(range(RING)):
        local_in[block] = state
        sig_state, sig_slope = line_of(rows_x, block, 2), line_of(rows_x, block, 3)
        res_sum = res_sum + line_of(rows_x, block, 4) + state * sig_state
        dec_sum = dec_sum + line_of(rows_x, block, 5) + slope * sig_state + state * sig_slope
        skip_sum = skip_sum + line_of(rows_x, block, 6)
        slope = line_of(rows_x, block, 1) + jump * (slope + tokens * state)
        state = line_of(rows_x, block, 0) + jump * state
    sig_state, sig_slope = empty, empty
    for block in range(RING):
        sig_slope = line_of(rows_x, block, 3) + jump * (sig_slope + tokens * sig_state)
        sig_state = line_of(rows_x, block, 2) + jump * sig_state
    for line, part in enumerate((state, slope, sig_state, sig_slope, res_sum, dec_sum, skip_sum, jump)):
        rows_z[z, pl.ds(line, share, stride=8), :] = part

    def z_copy(step):
        return pltpu.make_async_remote_copy(
            src_ref=rows_z.at[z], dst_ref=rows_z.at[z],
            send_sem=z_ss.at[step], recv_sem=z_rs.at[step],
            device_id=at_z(step), device_id_type=MESH,
        )

    for step in range(1, RING):
        z_copy(step).start()
    for step in range(1, RING):
        z_copy(step).wait_recv()

    row_jump = jump * jump
    row_jump = row_jump * row_jump
    row_jump = row_jump * row_jump
    state, slope, res_sum, dec_sum, skip_sum, incoming = (empty,) * 6
    for row in reversed(range(RING)):
        incoming = jnp.where(z == row, state, incoming)
        sig_state, sig_slope = line_of(rows_z, row, 2), line_of(rows_z, row, 3)
        res_sum = res_sum + line_of(rows_z, row, 4) + state * sig_state
        dec_sum = dec_sum + line_of(rows_z, row, 5) + slope * sig_state + state * sig_slope
        skip_sum = skip_sum + line_of(rows_z, row, 6)
        slope = line_of(rows_z, row, 1) + row_jump * (slope + (tokens * RING) * state)
        state = line_of(rows_z, row, 0) + row_jump * state
    for block in reversed(range(RING)):
        back[block, 0:share, :] = local_in[block] + incoming
        back[block, share : 2 * share, :] = res_sum
        back[block, 2 * share : 3 * share, :] = dec_sum
        back[block, 3 * share : 4 * share, :] = skip_sum
        incoming = incoming * jump

    def b_copy(step):
        return pltpu.make_async_remote_copy(
            src_ref=back.at[lax.rem(x + step, RING)], dst_ref=full.at[x],
            send_sem=b_ss.at[step], recv_sem=b_rs.at[step],
            device_id=at_x(step), device_id_type=MESH,
        )

    for step in range(1, RING):
        b_copy(step).start()
    full[x] = back[x]
    for step in range(1, RING):
        b_copy(step).wait_recv()

    per_half = RING // 2
    for peer in range(RING):
        first, cols = (peer % per_half) * share, pl.ds((peer // per_half) * lanes, lanes)
        modes_here = pl.ds(first, share)
        state_in[modes_here, cols] = full[peer, 0:share, :]
        res_o[modes_here, cols] = full[peer, share : 2 * share, :] * (1.0 / length)
        dec_o[modes_here, cols] = full[peer, 2 * share : 3 * share, :] * (-1.0 / length) * (1.0 / length)
        if peer % per_half == 0:
            skip_o[:, cols] = full[peer, 3 * share : 3 * share + 1, :] * (1.0 / length**0.5)
    dec_o[...] = dec_o[...] * res_v[...]

    def late_steps(group, term):
        for step in range(8):
            pos = tokens - 1 - (group * 8 + step)
            term = term * pole
            here = pl.ds(pos, 1)
            yl[here, :] = yl[here, :] + jnp.sum(term, axis=0, keepdims=True)
        return term

    lax.fori_loop(0, tokens // 8, late_steps, gain * state_in[...])
    out[...] = (yl[...] + skip_v[...] * gc[...]).astype(BF16)

    for index in range(RING):
        pair_copy(index).wait_send()
    for slot in range(SLOTS):
        for way in (0, 1):
            ring_copy(way, slot).wait_send()
    for step in range(1, RING):
        x_copy(step).wait_send()
        z_copy(step).wait_send()
        b_copy(step).wait_send()


def body(signal, upstream, out_weight, residues, decays, skip_gain):
    tokens, width = signal.shape
    features = upstream.shape[1]
    modes = residues.shape[1]
    lanes = width // 2
    share = 2 * modes // RING
    any_ref = pl.BlockSpec(memory_space=pl.ANY)
    in_vmem = pl.BlockSpec(memory_space=pltpu.VMEM)
    dma = pltpu.SemaphoreType.DMA
    grad_signal, res_t, dec_t, skip = pl.pallas_call(
        kernel,
        out_shape=(
            jax.ShapeDtypeStruct((tokens, width), BF16),
            jax.ShapeDtypeStruct((modes, width), F32),
            jax.ShapeDtypeStruct((modes, width), F32),
            jax.ShapeDtypeStruct((1, width), F32),
        ),
        in_specs=[any_ref] * 6,
        out_specs=(in_vmem,) * 4,
        scratch_shapes=[
            pltpu.VMEM((tokens, width), BF16),
            pltpu.VMEM((tokens, features), BF16),
            pltpu.VMEM((RING, 2 * width, features), BF16),
            pltpu.VMEM((modes, width), F32),
            pltpu.VMEM((modes, width), F32),
            pltpu.VMEM((1, width), F32),
            pltpu.VMEM((tokens, width), F32),
            pltpu.VMEM((RING, tokens, width), BF16),
            pltpu.VMEM((RING, tokens, width), BF16),
            pltpu.VMEM((RING, tokens, width), F32),
            pltpu.VMEM((2, SLOTS, tokens // 2, width), BF16),
            pltpu.VMEM((2, SLOTS, tokens // 2, width), BF16),
            pltpu.VMEM((tokens, width), F32),
            pltpu.VMEM((tokens, width), F32),
            pltpu.VMEM((2 * modes * 8, lanes), F32),
            pltpu.VMEM((RING, share * 8, lanes), F32),
            pltpu.VMEM((RING, share * 8, lanes), F32),
            pltpu.VMEM((RING, share, lanes), F32),
            pltpu.VMEM((RING, share * 4, lanes), F32),
            pltpu.VMEM((RING, share * 4, lanes), F32),
            pltpu.VMEM((modes, width), F32),
            dma((5,)), dma((RING,)), dma((RING,)), dma((RING,)),
            dma((2, SLOTS)), dma((2, SLOTS)),
            dma((RING,)), dma((RING,)), dma((RING,)), dma((RING,)), dma((RING,)), dma((RING,)),
        ],
        compiler_params=pltpu.CompilerParams(collective_id=0, has_side_effects=True),
    )(signal, upstream, out_weight, residues.T, decays.T, skip_gain.reshape(1, width))
    return grad_signal, res_t.T, dec_t.T, skip.reshape(width)


def solution(mesh):
    placed = (P("ctx", "ch"), P("ctx", "ch"), P(None, "ch"), P("ch", None), P("ch", None), P("ch"))
    return jax.shard_map(
        body,
        mesh=mesh,
        in_specs=placed,
        out_specs=(P("ctx", "ch"), P("ch", None), P("ch", None), P("ch")),
        check_vma=False,
    )
```

```python
import functools

import jax
import jax.numpy as jnp
from jax import lax
from jax.experimental import pallas as pl
from jax.experimental.pallas import tpu as pltpu
from jax.sharding import PartitionSpec as P

MESH = pl.DeviceIdType.MESH
F32 = jnp.float32
BF16 = jnp.bfloat16
RING = 8
FAR_WAY = ((4, 1), (4, 0), (3, 1), (3, 0), (2, 1), (2, 0), (1, 1), (1, 0))
NEAR_WAY = FAR_WAY[2:]
SENDS = len(FAR_WAY) + len(NEAR_WAY)


def kernel(
    sig_h, up_h, w_h, res_h, dec_h, skip_h,
    base_o, small_o,
    sig_v, up_v, w_v, res_v, dec_v, skip_v,
    sig_f, pair_s, pair_r, own, ring_s, ring_r, gc, yl,
    early_s, late_s, early_x, late_x, early_z, late_z, jumps, local_in, back, full,
    local_sem, w_sem, pair_ss, pair_rs, ring_ss, ring_rs,
    xe_ss, xe_rs, xl_ss, xl_rs, ze_ss, ze_rs, zl_ss, zl_rs, b_ss, b_rs,
):
    tokens, width = sig_h.shape
    half_rows = tokens // 2
    lanes = width // 2
    modes = res_h.shape[0]
    share = 2 * modes // RING
    per_half = RING // 2
    length = tokens * RING * RING
    ctx = lax.axis_index("ctx")
    ch = lax.axis_index("ch")
    z, x = lax.div(ctx, RING), lax.rem(ctx, RING)
    y, core = lax.div(ch, 2), lax.rem(ch, 2)

    def at_x(step):
        return (z * RING + lax.rem(x + step, RING), ch)

    def at_z(step):
        return (lax.rem(z + step, RING) * RING + x, ch)

    def at_y(step):
        return (ctx, lax.rem(y + step, RING) * 2 + core)

    partner = (ctx, y * 2 + 1 - core)
    up_ring = 1 + core * (RING - 2)

    barrier = pltpu.get_barrier_semaphore()
    peers = [partner, at_y(1), at_y(RING - 1)]
    peers += [at_x(step) for step in range(1, RING)] + [at_z(step) for step in range(1, RING)]
    for peer in peers:
        pl.semaphore_signal(barrier, inc=1, device_id=peer, device_id_type=MESH)

    def w_copy(index):
        offset = (index + 1) // 2
        dest = lax.rem(y + (4 - offset if index % 2 else 4 + offset), RING)
        return pltpu.make_async_copy(
            w_h.at[pl.ds(dest * 2 * width, 2 * width), :], w_v.at[index], w_sem.at[index]
        )

    loads = [
        pltpu.make_async_copy(src, dst, local_sem.at[n])
        for n, (src, dst) in enumerate(
            ((up_h, up_v), (dec_h, dec_v), (res_h, res_v), (skip_h, skip_v), (sig_h, sig_v))
        )
    ]
    loads[0].start()
    w_copy(0).start()
    w_copy(1).start()
    for load in loads[1:]:
        load.start()
    for index in range(2, RING):
        w_copy(index).start()
    for load in loads:
        load.wait()
    pole = jnp.exp(dec_v[...] * (-1.0 / length))
    pole_block = jnp.exp(dec_v[...] * (-float(tokens) / length))
    gain = res_v[...] * (1.0 / length**0.5)
    small_o[pl.ds(modes, modes), :] = pole
    sig_f[...] = sig_v[...].astype(F32)
    zero = jnp.zeros((modes, width), F32)

    def piece(part, peer):
        first, cols = (peer % per_half) * share, (peer // per_half) * lanes
        return part[first : first + share, cols : cols + lanes]

    for peer in range(RING):
        jumps[peer, 0:share, :] = piece(pole_block, peer)
    pl.semaphore_wait(barrier, len(peers))

    def pair_copy(index):
        return pltpu.make_async_remote_copy(
            src_ref=pair_s.at[index], dst_ref=pair_r.at[index],
            send_sem=pair_ss.at[index], recv_sem=pair_rs.at[index],
            device_id=partner, device_id_type=MESH,
        )

    def product(index):
        w_copy(index).wait()
        for mine in (0, 1):
            side = lax.rem(core + 1 + mine, 2) * width
            part = lax.dot_general(
                up_v[...], w_v[index, pl.ds(pl.multiple_of(side, width), width), :],
                (((1,), (1,)), ((), ())), preferred_element_type=F32,
            )
            if mine:
                own[index] = part
            else:
                pair_s[index] = part.astype(BF16)
                pair_copy(index).start()

    def ring_copy(far, send):
        slot = send if far else send + len(FAR_WAY)
        return pltpu.make_async_remote_copy(
            src_ref=ring_s.at[slot], dst_ref=ring_r.at[slot],
            send_sem=ring_ss.at[slot], recv_sem=ring_rs.at[slot],
            device_id=at_y(up_ring if far else RING - up_ring), device_id_type=MESH,
        )

    arrived = set()

    def chip_sum(far, dist, half):
        if dist == 0:
            index = RING - 1
        elif dist == per_half:
            index = 0
        else:
            index = 2 * (per_half - dist) + (core - 1 if far else -core)
        if (far, dist) not in arrived:
            arrived.add((far, dist))
            pair_copy(index).wait_recv()
        span = pl.ds(half * half_rows, half_rows)
        return own[index, span, :] + pair_r[index, span, :].astype(F32)

    def incoming_sum(far, send):
        ring_copy(far, send).wait_recv()
        return ring_r[send if far else send + len(FAR_WAY)].astype(F32)

    def ring_send(far, send):
        dist, half = (FAR_WAY if far else NEAR_WAY)[send]
        total = chip_sum(far, dist, half)
        if send >= 2:
            total = total + incoming_sum(far, send - 2)
        ring_s[send if far else send + len(FAR_WAY)] = total.astype(BF16)
        ring_copy(far, send).start()

    product(0)
    product(1)
    product(2)
    ring_send(True, 0)
    ring_send(True, 1)
    product(3)
    product(4)
    ring_send(False, 0)
    ring_send(False, 1)
    product(5)
    product(6)
    product(7)

    def signal_steps(group, carry):
        state, slope = carry
        for step in range(8):
            row = sig_f[pl.ds(group * 8 + step, 1), :]
            state = (state + row) * pole
            slope = slope * pole + state
        return state, slope

    sig_state, sig_slope = lax.fori_loop(0, tokens // 8, signal_steps, (zero, zero))
    for peer in range(RING):
        early_s[peer] = jnp.concatenate([piece(sig_state, peer), piece(sig_slope, peer)], axis=0)

    def x_copy(step, early):
        peer = lax.rem(x + step, RING)
        src, dst, ss, rs = (early_s, early_x, xe_ss, xe_rs) if early else (late_s, late_x, xl_ss, xl_rs)
        return pltpu.make_async_remote_copy(
            src_ref=src.at[peer], dst_ref=dst.at[x], send_sem=ss.at[step], recv_sem=rs.at[step],
            device_id=at_x(step), device_id_type=MESH,
        )

    def z_copy(step, early):
        ref, ss, rs = (early_z, ze_ss, ze_rs) if early else (late_z, zl_ss, zl_rs)
        return pltpu.make_async_remote_copy(
            src_ref=ref.at[z], dst_ref=ref.at[z], send_sem=ss.at[step], recv_sem=rs.at[step],
            device_id=at_z(step), device_id_type=MESH,
        )

    for step in range(1, RING):
        x_copy(step, True).start()
    early_x[x] = early_s[x]

    ring_send(True, 2)
    ring_send(True, 3)
    ring_send(False, 2)
    ring_send(False, 3)
    ring_send(True, 4)
    ring_send(True, 5)
    ring_send(False, 4)
    ring_send(False, 5)

    for step in range(1, RING):
        x_copy(step, True).wait_recv()
    jump = jumps[x, 0:share, :]
    empty = jnp.zeros((share, lanes), F32)
    sig_state, sig_slope = empty, empty
    for block in range(RING):
        sig_slope = early_x[block, share : 2 * share, :] + jump * (sig_slope + tokens * sig_state)
        sig_state = early_x[block, 0:share, :] + jump * sig_state
    early_z[z] = jnp.concatenate([sig_state, sig_slope], axis=0)
    for step in range(1, RING):
        z_copy(step, True).start()

    ring_send(True, 6)
    ring_send(True, 7)

    def gradient_steps(last, group, carry):
        state, slope, res_sum, dec_sum = carry
        for step in range(8):
            pos = last - (group * 8 + step)
            grad = gc[pl.ds(pos, 1), :]
            row = sig_f[pl.ds(pos, 1), :]
            moved = state * pole
            state = grad + moved
            slope = slope * pole + moved
            res_sum = res_sum + row * state
            dec_sum = dec_sum + row * slope
            yl[pl.ds(pos, 1), :] = jnp.sum(gain * state, axis=0, keepdims=True)
        return state, slope, res_sum, dec_sum

    carry = (zero, zero, zero, zero)
    skip_sum = jnp.zeros((1, width), F32)
    for half in (1, 0):
        total = chip_sum(None, 0, half)
        for far, way in ((False, NEAR_WAY), (True, FAR_WAY)):
            total = total + incoming_sum(far, len(way) - 1 - half)
        total = total.astype(BF16).astype(F32)
        span = pl.ds(half * half_rows, half_rows)
        gc[span, :] = total
        skip_sum = skip_sum + jnp.sum(total * sig_f[span, :], axis=0, keepdims=True)
        carry = lax.fori_loop(
            0, half_rows // 8, functools.partial(gradient_steps, (half + 1) * half_rows - 1), carry
        )
    state, slope, res_sum, dec_sum = carry

    skip_rows = jnp.broadcast_to(skip_sum, (8, width))
    for peer in range(RING):
        cols = (peer // per_half) * lanes
        late_s[peer, 0:8, :] = jnp.concatenate([piece(state, peer), piece(slope, peer)], axis=0).astype(BF16)
        late_s[peer, 8:16, :] = jnp.concatenate([piece(res_sum, peer), piece(dec_sum, peer)], axis=0).astype(BF16)
        late_s[peer, 16:24, :] = skip_rows[:, cols : cols + lanes].astype(BF16)
    for step in range(1, RING):
        x_copy(step, False).start()
    late_x[x] = late_s[x]
    yl[...] = yl[...] + skip_v[...] * gc[...]
    base_copy = pltpu.make_async_copy(yl, base_o, local_sem.at[len(loads)])
    base_copy.start()
    for step in range(1, RING):
        x_copy(step, False).wait_recv()

    def parts_of(early, late, index):
        sums = late[index].astype(F32)
        early_part = early[index]
        return (
            sums[0:share], sums[share : 2 * share], sums[2 * share : 3 * share], sums[3 * share : 4 * share],
            sums[4 * share : 5 * share], early_part[0:share], early_part[share : 2 * share],
        )

    def join(parts, carry, jump, span):
        own_state, own_slope, own_res, own_dec, own_skip, sig_state, sig_slope = parts
        state, slope, res_sum, dec_sum, skip_sum = carry
        return (
            own_state + jump * state,
            own_slope + jump * (slope + span * state),
            res_sum + own_res + state * sig_state,
            dec_sum + own_dec + slope * sig_state + state * sig_slope,
            skip_sum + own_skip,
        )

    carry = (empty,) * 5
    for block in reversed(range(RING)):
        local_in[block] = carry[0]
        carry = join(parts_of(early_x, late_x, block), carry, jump, float(tokens))
    late_z[z, 0:8, :] = jnp.concatenate(carry[0:2], axis=0).astype(BF16)
    late_z[z, 8:16, :] = jnp.concatenate(carry[2:4], axis=0).astype(BF16)
    late_z[z, 16:24, :] = jnp.concatenate([carry[4], carry[4]], axis=0).astype(BF16)
    for step in range(1, RING):
        z_copy(step, False).start()
    row_jump = jump * jump
    row_jump = row_jump * row_jump
    row_jump = row_jump * row_jump
    for step in range(1, RING):
        z_copy(step, True).wait_recv()
    for step in range(1, RING):
        z_copy(step, False).wait_recv()

    incoming = empty
    carry = (empty,) * 5
    for row in reversed(range(RING)):
        incoming = jnp.where(z == row, carry[0], incoming)
        carry = join(parts_of(early_z, late_z, row), carry, row_jump, float(tokens * RING))
    for block in reversed(range(RING)):
        back[block, 0:8, :] = jnp.concatenate([local_in[block] + incoming, carry[2]], axis=0)
        back[block, 8:16, :] = jnp.concatenate([carry[3], carry[4]], axis=0)
        incoming = incoming * jump

    def b_copy(step):
        return pltpu.make_async_remote_copy(
            src_ref=back.at[lax.rem(x + step, RING)], dst_ref=full.at[x],
            send_sem=b_ss.at[step], recv_sem=b_rs.at[step],
            device_id=at_x(step), device_id_type=MESH,
        )

    for step in range(1, RING):
        b_copy(step).start()
    full[x] = back[x]
    base_copy.wait()
    for index in range(RING):
        pair_copy(index).wait_send()
    for far, way in ((True, FAR_WAY), (False, NEAR_WAY)):
        for send in range(len(way)):
            ring_copy(far, send).wait_send()
    for step in range(1, RING):
        for early in (True, False):
            x_copy(step, early).wait_send()
            z_copy(step, early).wait_send()
    for step in range(1, RING):
        b_copy(step).wait_recv()

    for peer in range(RING):
        cols = pl.ds((peer // per_half) * lanes, lanes)
        first = (peer % per_half) * share
        for line in range(3):
            small_o[pl.ds((0, 2, 3)[line] * modes + first, share), cols] = full[
                peer, line * share : (line + 1) * share, :
            ]
        if peer % per_half == 0:
            small_o[pl.ds(4 * modes, 8), cols] = full[peer, 8:16, :]
    here = pl.ds(0, modes)
    small_o[here, :] = small_o[here, :] * gain
    here = pl.ds(2 * modes, modes)
    small_o[here, :] = small_o[here, :] * (1.0 / length)
    here = pl.ds(3 * modes, modes)
    small_o[here, :] = small_o[here, :] * (-1.0 / length) * (1.0 / length) * res_v[...]
    here = pl.ds(4 * modes, 8)
    small_o[here, :] = small_o[here, :] * (1.0 / length**0.5)
    for step in range(1, RING):
        b_copy(step).wait_send()


def finish(base, small, out, res_o, dec_o, skip_o, late):
    tokens = base.shape[0]
    modes = res_o.shape[0]
    res_o[...] = small[pl.ds(2 * modes, modes), :]
    dec_o[...] = small[pl.ds(3 * modes, modes), :]
    skip_o[...] = small[pl.ds(4 * modes + 4, 1), :]
    pole = small[pl.ds(modes, modes), :]

    def late_steps(group, term):
        for step in range(8):
            term = term * pole
            late[pl.ds(tokens - 1 - (group * 8 + step), 1), :] = jnp.sum(term, axis=0, keepdims=True)
        return term

    lax.fori_loop(0, tokens // 8, late_steps, small[pl.ds(0, modes), :])
    out[...] = (base[...] + late[...]).astype(BF16)


def body(signal, upstream, out_weight, residues, decays, skip_gain):
    tokens, width = signal.shape
    features = upstream.shape[1]
    modes = residues.shape[1]
    lanes = width // 2
    share = 2 * modes // RING
    any_ref = pl.BlockSpec(memory_space=pl.ANY)
    in_vmem = pl.BlockSpec(memory_space=pltpu.VMEM)
    dma = pltpu.SemaphoreType.DMA
    base, small = pl.pallas_call(
        kernel,
        out_shape=(
            jax.ShapeDtypeStruct((tokens, width), F32),
            jax.ShapeDtypeStruct((4 * modes + 8, width), F32),
        ),
        in_specs=[any_ref] * 6,
        out_specs=(any_ref, in_vmem),
        scratch_shapes=[
            pltpu.VMEM((tokens, width), BF16),
            pltpu.VMEM((tokens, features), BF16),
            pltpu.VMEM((RING, 2 * width, features), BF16),
            pltpu.VMEM((modes, width), F32),
            pltpu.VMEM((modes, width), F32),
            pltpu.VMEM((1, width), F32),
            pltpu.VMEM((tokens, width), F32),
            pltpu.VMEM((RING, tokens, width), BF16),
            pltpu.VMEM((RING, tokens, width), BF16),
            pltpu.VMEM((RING, tokens, width), F32),
            pltpu.VMEM((SENDS, tokens // 2, width), BF16),
            pltpu.VMEM((SENDS, tokens // 2, width), BF16),
            pltpu.VMEM((tokens, width), F32),
            pltpu.VMEM((tokens, width), F32),
            pltpu.VMEM((RING, 2 * share, lanes), F32),
            pltpu.VMEM((RING, 6 * share, lanes), BF16),
            pltpu.VMEM((RING, 2 * share, lanes), F32),
            pltpu.VMEM((RING, 6 * share, lanes), BF16),
            pltpu.VMEM((RING, 2 * share, lanes), F32),
            pltpu.VMEM((RING, 6 * share, lanes), BF16),
            pltpu.VMEM((RING, 2 * share, lanes), F32),
            pltpu.VMEM((RING, share, lanes), F32),
            pltpu.VMEM((RING, 4 * share, lanes), F32),
            pltpu.VMEM((RING, 4 * share, lanes), F32),
            dma((6,)), dma((RING,)), dma((RING,)), dma((RING,)), dma((SENDS,)), dma((SENDS,)),
        ] + [dma((RING,))] * 10,
        compiler_params=pltpu.CompilerParams(collective_id=0, has_side_effects=True),
    )(signal, upstream, out_weight, residues.T, decays.T, skip_gain.reshape(1, width))
    grad_signal, res_t, dec_t, skip = pl.pallas_call(
        finish,
        out_shape=(
            jax.ShapeDtypeStruct((tokens, width), BF16),
            jax.ShapeDtypeStruct((modes, width), F32),
            jax.ShapeDtypeStruct((modes, width), F32),
            jax.ShapeDtypeStruct((1, width), F32),
        ),
        in_specs=[in_vmem] * 2,
        out_specs=(in_vmem,) * 4,
        scratch_shapes=[pltpu.VMEM((tokens, width), F32)],
    )(base, small)
    return grad_signal, res_t.T, dec_t.T, skip.reshape(width)


def solution(mesh):
    placed = (P("ctx", "ch"), P("ctx", "ch"), P(None, "ch"), P("ch", None), P("ch", None), P("ch"))
    return jax.shard_map(
        body,
        mesh=mesh,
        in_specs=placed,
        out_specs=(P("ctx", "ch"), P("ch", None), P("ch", None), P("ch")),
        check_vma=False,
    )
```

```python
import functools

import jax
import jax.numpy as jnp
from jax import lax
from jax.experimental import pallas as pl
from jax.experimental.pallas import tpu as pltpu
from jax.sharding import PartitionSpec as P

MESH = pl.DeviceIdType.MESH
F32 = jnp.float32
BF16 = jnp.bfloat16
RING = 8
PARTS = 4
PEER_ORDER = (4, 3, 5, 2, 6, 1, 7)
FAR_WAY = tuple((dist, part) for dist in (4, 3, 2, 1) for part in reversed(range(PARTS)))
NEAR_WAY = FAR_WAY[PARTS:]
SENDS = len(FAR_WAY) + len(NEAR_WAY)


def kernel(
    sig_h, up_h, w_h, res_h, dec_h, skip_h,
    base_o, small_o,
    sig_v, up_v, w_v, res_v, dec_v, skip_v,
    sig_f, pair_s, pair_r, own, ring_s, ring_r, gc, yl,
    early_s, late_s, early_x, late_x, early_z, late_z, jumps, local_in, back, full,
    local_sem, w_sem, pair_ss, pair_rs, ring_ss, ring_rs,
    xe_ss, xe_rs, xl_ss, xl_rs, ze_ss, ze_rs, zl_ss, zl_rs, b_ss, b_rs,
):
    tokens, width = sig_h.shape
    part_rows = tokens // PARTS
    lanes = width // 2
    modes = res_h.shape[0]
    share = 2 * modes // RING
    per_half = RING // 2
    length = tokens * RING * RING
    ctx = lax.axis_index("ctx")
    ch = lax.axis_index("ch")
    z, x = lax.div(ctx, RING), lax.rem(ctx, RING)
    y, core = lax.div(ch, 2), lax.rem(ch, 2)

    def at_x(step):
        return (z * RING + lax.rem(x + step, RING), ch)

    def at_z(step):
        return (lax.rem(z + step, RING) * RING + x, ch)

    def at_y(step):
        return (ctx, lax.rem(y + step, RING) * 2 + core)

    partner = (ctx, y * 2 + 1 - core)
    up_ring = 1 + core * (RING - 2)

    barrier = pltpu.get_barrier_semaphore()
    peers = [partner, at_y(1), at_y(RING - 1)]
    peers += [at_x(step) for step in range(1, RING)] + [at_z(step) for step in range(1, RING)]
    for peer in peers:
        pl.semaphore_signal(barrier, inc=1, device_id=peer, device_id_type=MESH)

    def w_copy(index):
        offset = (index + 1) // 2
        dest = lax.rem(y + (4 - offset if index % 2 else 4 + offset), RING)
        return pltpu.make_async_copy(
            w_h.at[pl.ds(dest * 2 * width, 2 * width), :], w_v.at[index], w_sem.at[index]
        )

    loads = [
        pltpu.make_async_copy(src, dst, local_sem.at[n])
        for n, (src, dst) in enumerate(
            ((up_h, up_v), (dec_h, dec_v), (res_h, res_v), (skip_h, skip_v), (sig_h, sig_v))
        )
    ]
    loads[0].start()
    w_copy(0).start()
    w_copy(1).start()
    for load in loads[1:]:
        load.start()
    for index in range(2, RING):
        w_copy(index).start()
    for load in loads:
        load.wait()
    pole = jnp.exp(dec_v[...] * (-1.0 / length))
    pole_block = jnp.exp(dec_v[...] * (-float(tokens) / length))
    gain = res_v[...] * (1.0 / length**0.5)
    small_o[pl.ds(modes, modes), :] = pole
    sig_f[...] = sig_v[...].astype(F32)
    zero = jnp.zeros((modes, width), F32)

    def piece(part, peer):
        first, cols = (peer % per_half) * share, (peer // per_half) * lanes
        return part[first : first + share, cols : cols + lanes]

    for peer in range(RING):
        jumps[peer, 0:share, :] = piece(pole_block, peer)

    def pair_copy(index):
        return pltpu.make_async_remote_copy(
            src_ref=pair_s.at[index], dst_ref=pair_r.at[index],
            send_sem=pair_ss.at[index], recv_sem=pair_rs.at[index],
            device_id=partner, device_id_type=MESH,
        )

    def product(index):
        w_copy(index).wait()
        for mine in (0, 1):
            side = lax.rem(core + 1 + mine, 2) * width
            part = lax.dot_general(
                up_v[...], w_v[index, pl.ds(pl.multiple_of(side, width), width), :],
                (((1,), (1,)), ((), ())), preferred_element_type=F32,
            )
            if mine:
                own[index] = part
            else:
                pair_s[index] = part.astype(BF16)
                if index > 0:
                    pair_copy(index).start()

    def ring_copy(far, send):
        slot = send if far else send + len(FAR_WAY)
        return pltpu.make_async_remote_copy(
            src_ref=ring_s.at[slot], dst_ref=ring_r.at[slot],
            send_sem=ring_ss.at[slot], recv_sem=ring_rs.at[slot],
            device_id=at_y(up_ring if far else RING - up_ring), device_id_type=MESH,
        )

    arrived = set()

    def chip_sum(far, dist, part):
        if dist == 0:
            index = RING - 1
        elif dist == per_half:
            index = 0
        else:
            index = 2 * (per_half - dist) + (core - 1 if far else -core)
        if (far, dist) not in arrived:
            arrived.add((far, dist))
            pair_copy(index).wait_recv()
        span = pl.ds(part * part_rows, part_rows)
        return own[index, span, :] + pair_r[index, span, :].astype(F32)

    def incoming_sum(far, send):
        ring_copy(far, send).wait_recv()
        return ring_r[send if far else send + len(FAR_WAY)].astype(F32)

    def ring_send(far, send):
        dist, part = (FAR_WAY if far else NEAR_WAY)[send]
        total = chip_sum(far, dist, part)
        if send >= PARTS:
            total = total + incoming_sum(far, send - PARTS)
        ring_s[send if far else send + len(FAR_WAY)] = total.astype(BF16)
        ring_copy(far, send).start()

    def signal_steps(group, carry):
        state, slope = carry
        for step in range(8):
            row = sig_f[pl.ds(group * 8 + step, 1), :]
            state = (state + row) * pole
            slope = slope * pole + state
        return state, slope

    def signal_part(part, carry):
        groups = tokens // 8 // 4
        return lax.fori_loop(part * groups, (part + 1) * groups, signal_steps, carry)

    def x_copy(step, early):
        peer = lax.rem(x + step, RING)
        src, dst, ss, rs = (early_s, early_x, xe_ss, xe_rs) if early else (late_s, late_x, xl_ss, xl_rs)
        return pltpu.make_async_remote_copy(
            src_ref=src.at[peer], dst_ref=dst.at[x], send_sem=ss.at[step], recv_sem=rs.at[step],
            device_id=at_x(step), device_id_type=MESH,
        )

    def z_copy(step, early):
        ref, ss, rs = (early_z, ze_ss, ze_rs) if early else (late_z, zl_ss, zl_rs)
        return pltpu.make_async_remote_copy(
            src_ref=ref.at[z], dst_ref=ref.at[z], send_sem=ss.at[step], recv_sem=rs.at[step],
            device_id=at_z(step), device_id_type=MESH,
        )

    product(0)
    pl.semaphore_wait(barrier, len(peers))
    pair_copy(0).start()
    product(1)
    product(2)
    for send in range(PARTS):
        ring_send(True, send)
    product(3)
    product(4)
    for send in range(PARTS):
        ring_send(False, send)
    product(5)
    product(6)
    product(7)
    signal = signal_part(0, (zero, zero))
    for send in range(PARTS, 3 * PARTS):
        ring_send(True, send)
        ring_send(False, send)
        if send == PARTS + 1:
            signal = signal_part(1, signal)
        if send == 2 * PARTS - 1:
            signal = signal_part(2, signal)
        if send == 2 * PARTS + 1:
            signal = signal_part(3, signal)
            for peer in range(RING):
                early_s[peer] = jnp.concatenate([piece(signal[0], peer), piece(signal[1], peer)], axis=0)
            for step in PEER_ORDER:
                x_copy(step, True).start()
    early_x[x] = early_s[x]
    for send in range(3 * PARTS, 4 * PARTS):
        ring_send(True, send)

    def gradient_steps(last, group, carry):
        state, slope, res_sum, dec_sum = carry
        for step in range(8):
            pos = last - (group * 8 + step)
            grad = gc[pl.ds(pos, 1), :]
            row = sig_f[pl.ds(pos, 1), :]
            moved = state * pole
            state = grad + moved
            slope = slope * pole + moved
            res_sum = res_sum + row * state
            dec_sum = dec_sum + row * slope
            yl[pl.ds(pos, 1), :] = jnp.sum(gain * state, axis=0, keepdims=True)
        return state, slope, res_sum, dec_sum

    carry = (zero, zero, zero, zero)
    skip_sum = jnp.zeros((1, width), F32)
    for part in reversed(range(PARTS)):
        total = chip_sum(None, 0, part)
        for far, way in ((False, NEAR_WAY), (True, FAR_WAY)):
            total = total + incoming_sum(far, len(way) - 1 - part)
        total = total.astype(BF16).astype(F32)
        span = pl.ds(part * part_rows, part_rows)
        gc[span, :] = total
        skip_sum = skip_sum + jnp.sum(total * sig_f[span, :], axis=0, keepdims=True)
        carry = lax.fori_loop(
            0, part_rows // 8, functools.partial(gradient_steps, (part + 1) * part_rows - 1), carry
        )
    state, slope, res_sum, dec_sum = carry

    skip_rows = jnp.broadcast_to(skip_sum, (8, width))
    for peer in range(RING):
        cols = (peer // per_half) * lanes
        late_s[peer, 0:8, :] = jnp.concatenate([piece(state, peer), piece(slope, peer)], axis=0).astype(BF16)
        late_s[peer, 8:16, :] = jnp.concatenate([piece(res_sum, peer), piece(dec_sum, peer)], axis=0).astype(BF16)
        late_s[peer, 16:24, :] = skip_rows[:, cols : cols + lanes].astype(BF16)
    for step in PEER_ORDER:
        x_copy(step, False).start()
    late_x[x] = late_s[x]

    for step in range(1, RING):
        x_copy(step, True).wait_recv()
    jump = jumps[x, 0:share, :]
    empty = jnp.zeros((share, lanes), F32)
    sig_state, sig_slope = empty, empty
    for block in range(RING):
        sig_slope = early_x[block, share : 2 * share, :] + jump * (sig_slope + tokens * sig_state)
        sig_state = early_x[block, 0:share, :] + jump * sig_state
    early_z[z] = jnp.concatenate([sig_state, sig_slope], axis=0)
    for step in PEER_ORDER:
        z_copy(step, True).start()
    yl[...] = yl[...] + skip_v[...] * gc[...]
    base_copy = pltpu.make_async_copy(yl, base_o, local_sem.at[len(loads)])
    base_copy.start()
    for step in range(1, RING):
        x_copy(step, False).wait_recv()

    def parts_of(early, late, index):
        sums = late[index].astype(F32)
        early_part = early[index]
        return (
            sums[0:share], sums[share : 2 * share], sums[2 * share : 3 * share], sums[3 * share : 4 * share],
            sums[4 * share : 5 * share], early_part[0:share], early_part[share : 2 * share],
        )

    def join(parts, carry, jump, span):
        own_state, own_slope, own_res, own_dec, own_skip, sig_state, sig_slope = parts
        state, slope, res_sum, dec_sum, skip_sum = carry
        return (
            own_state + jump * state,
            own_slope + jump * (slope + span * state),
            res_sum + own_res + state * sig_state,
            dec_sum + own_dec + slope * sig_state + state * sig_slope,
            skip_sum + own_skip,
        )

    carry = (empty,) * 5
    for block in reversed(range(RING)):
        local_in[block] = carry[0]
        carry = join(parts_of(early_x, late_x, block), carry, jump, float(tokens))
    late_z[z, 0:8, :] = jnp.concatenate(carry[0:2], axis=0).astype(BF16)
    late_z[z, 8:16, :] = jnp.concatenate(carry[2:4], axis=0).astype(BF16)
    late_z[z, 16:24, :] = jnp.concatenate([carry[4], carry[4]], axis=0).astype(BF16)
    for step in PEER_ORDER:
        z_copy(step, False).start()
    row_jump = jump * jump
    row_jump = row_jump * row_jump
    row_jump = row_jump * row_jump
    for step in range(1, RING):
        z_copy(step, True).wait_recv()
    for step in range(1, RING):
        z_copy(step, False).wait_recv()

    incoming = empty
    carry = (empty,) * 5
    for row in reversed(range(RING)):
        incoming = jnp.where(z == row, carry[0], incoming)
        carry = join(parts_of(early_z, late_z, row), carry, row_jump, float(tokens * RING))
    for block in reversed(range(RING)):
        back[block, 0:8, :] = jnp.concatenate([local_in[block] + incoming, carry[2]], axis=0).astype(BF16)
        back[block, 8:16, :] = jnp.concatenate([carry[3], carry[4]], axis=0).astype(BF16)
        incoming = incoming * jump

    def b_copy(step):
        return pltpu.make_async_remote_copy(
            src_ref=back.at[lax.rem(x + step, RING)], dst_ref=full.at[x],
            send_sem=b_ss.at[step], recv_sem=b_rs.at[step],
            device_id=at_x(step), device_id_type=MESH,
        )

    for step in PEER_ORDER:
        b_copy(step).start()
    full[x] = back[x]
    base_copy.wait()
    for index in range(RING):
        pair_copy(index).wait_send()
    for far, way in ((True, FAR_WAY), (False, NEAR_WAY)):
        for send in range(len(way)):
            ring_copy(far, send).wait_send()
    for step in range(1, RING):
        for early in (True, False):
            x_copy(step, early).wait_send()
            z_copy(step, early).wait_send()
    for step in range(1, RING):
        b_copy(step).wait_recv()

    for peer in range(RING):
        cols = pl.ds((peer // per_half) * lanes, lanes)
        first = (peer % per_half) * share
        sums = full[peer].astype(F32)
        for line in range(3):
            small_o[pl.ds((0, 2, 3)[line] * modes + first, share), cols] = sums[line * share : (line + 1) * share]
        if peer % per_half == 0:
            small_o[pl.ds(4 * modes, 8), cols] = sums[2 * share : 4 * share]
    here = pl.ds(0, modes)
    small_o[here, :] = small_o[here, :] * gain
    here = pl.ds(2 * modes, modes)
    small_o[here, :] = small_o[here, :] * (1.0 / length)
    here = pl.ds(3 * modes, modes)
    small_o[here, :] = small_o[here, :] * (-1.0 / length) * (1.0 / length) * res_v[...]
    here = pl.ds(4 * modes, 8)
    small_o[here, :] = small_o[here, :] * (1.0 / length**0.5)
    for step in range(1, RING):
        b_copy(step).wait_send()


def finish(base, small, out, res_o, dec_o, skip_o, late):
    tokens = base.shape[0]
    modes = res_o.shape[0]
    res_o[...] = small[pl.ds(2 * modes, modes), :]
    dec_o[...] = small[pl.ds(3 * modes, modes), :]
    skip_o[...] = small[pl.ds(4 * modes + 4, 1), :]
    pole = small[pl.ds(modes, modes), :]

    def late_steps(group, term):
        for step in range(8):
            term = term * pole
            late[pl.ds(tokens - 1 - (group * 8 + step), 1), :] = jnp.sum(term, axis=0, keepdims=True)
        return term

    lax.fori_loop(0, tokens // 8, late_steps, small[pl.ds(0, modes), :])
    out[...] = (base[...] + late[...]).astype(BF16)


def body(signal, upstream, out_weight, residues, decays, skip_gain):
    tokens, width = signal.shape
    features = upstream.shape[1]
    modes = residues.shape[1]
    lanes = width // 2
    share = 2 * modes // RING
    any_ref = pl.BlockSpec(memory_space=pl.ANY)
    in_vmem = pl.BlockSpec(memory_space=pltpu.VMEM)
    dma = pltpu.SemaphoreType.DMA
    base, small = pl.pallas_call(
        kernel,
        out_shape=(
            jax.ShapeDtypeStruct((tokens, width), F32),
            jax.ShapeDtypeStruct((4 * modes + 8, width), F32),
        ),
        in_specs=[any_ref] * 6,
        out_specs=(any_ref, in_vmem),
        scratch_shapes=[
            pltpu.VMEM((tokens, width), BF16),
            pltpu.VMEM((tokens, features), BF16),
            pltpu.VMEM((RING, 2 * width, features), BF16),
            pltpu.VMEM((modes, width), F32),
            pltpu.VMEM((modes, width), F32),
            pltpu.VMEM((1, width), F32),
            pltpu.VMEM((tokens, width), F32),
            pltpu.VMEM((RING, tokens, width), BF16),
            pltpu.VMEM((RING, tokens, width), BF16),
            pltpu.VMEM((RING, tokens, width), F32),
            pltpu.VMEM((SENDS, tokens // PARTS, width), BF16),
            pltpu.VMEM((SENDS, tokens // PARTS, width), BF16),
            pltpu.VMEM((tokens, width), F32),
            pltpu.VMEM((tokens, width), F32),
            pltpu.VMEM((RING, 2 * share, lanes), F32),
            pltpu.VMEM((RING, 6 * share, lanes), BF16),
            pltpu.VMEM((RING, 2 * share, lanes), F32),
            pltpu.VMEM((RING, 6 * share, lanes), BF16),
            pltpu.VMEM((RING, 2 * share, lanes), F32),
            pltpu.VMEM((RING, 6 * share, lanes), BF16),
            pltpu.VMEM((RING, 2 * share, lanes), F32),
            pltpu.VMEM((RING, share, lanes), F32),
            pltpu.VMEM((RING, 4 * share, lanes), BF16),
            pltpu.VMEM((RING, 4 * share, lanes), BF16),
            dma((6,)), dma((RING,)), dma((RING,)), dma((RING,)), dma((SENDS,)), dma((SENDS,)),
        ] + [dma((RING,))] * 10,
        compiler_params=pltpu.CompilerParams(collective_id=0, has_side_effects=True),
    )(signal, upstream, out_weight, residues.T, decays.T, skip_gain.reshape(1, width))
    grad_signal, res_t, dec_t, skip = pl.pallas_call(
        finish,
        out_shape=(
            jax.ShapeDtypeStruct((tokens, width), BF16),
            jax.ShapeDtypeStruct((modes, width), F32),
            jax.ShapeDtypeStruct((modes, width), F32),
            jax.ShapeDtypeStruct((1, width), F32),
        ),
        in_specs=[in_vmem] * 2,
        out_specs=(in_vmem,) * 4,
        scratch_shapes=[pltpu.VMEM((tokens, width), F32)],
    )(base, small)
    return grad_signal, res_t.T, dec_t.T, skip.reshape(width)


def solution(mesh):
    placed = (P("ctx", "ch"), P("ctx", "ch"), P(None, "ch"), P("ch", None), P("ch", None), P("ch"))
    return jax.shard_map(
        body,
        mesh=mesh,
        in_specs=placed,
        out_specs=(P("ctx", "ch"), P("ch", None), P("ch", None), P("ch")),
        check_vma=False,
    )
```

```python
import functools

import jax
import jax.numpy as jnp
from jax import lax
from jax.experimental import pallas as pl
from jax.experimental.pallas import tpu as pltpu
from jax.sharding import PartitionSpec as P

MESH = pl.DeviceIdType.MESH
F32 = jnp.float32
BF16 = jnp.bfloat16
RING = 8
PARTS = 4
PEER_ORDER = (4, 3, 5, 2, 6, 1, 7)
FAR_WAY = tuple((dist, part) for dist in (4, 3, 2, 1) for part in reversed(range(PARTS)))
NEAR_WAY = FAR_WAY[PARTS:]
SENDS = len(FAR_WAY) + len(NEAR_WAY)


def kernel(
    sig_h, up_h, w_h, res_h, dec_h, skip_h,
    base_o, small_o,
    sig_v, up_v, w_v, res_v, dec_v, skip_v,
    sig_f, pair_s, pair_r, own, ring_s, ring_r, gc, yl,
    early_s, late_s, early_x, late_x, early_z, late_z, jumps, local_in, back, full,
    local_sem, w_sem, pair_ss, pair_rs, ring_ss, ring_rs,
    xe_ss, xe_rs, xl_ss, xl_rs, ze_ss, ze_rs, zl_ss, zl_rs, b_ss, b_rs,
):
    tokens, width = sig_h.shape
    part_rows = tokens // PARTS
    lanes = width // 2
    modes = res_h.shape[0]
    share = 2 * modes // RING
    per_half = RING // 2
    length = tokens * RING * RING
    ctx = lax.axis_index("ctx")
    ch = lax.axis_index("ch")
    z, x = lax.div(ctx, RING), lax.rem(ctx, RING)
    y, core = lax.div(ch, 2), lax.rem(ch, 2)

    def at_x(step):
        return (z * RING + lax.rem(x + step, RING), ch)

    def at_z(step):
        return (lax.rem(z + step, RING) * RING + x, ch)

    def at_y(step):
        return (ctx, lax.rem(y + step, RING) * 2 + core)

    partner = (ctx, y * 2 + 1 - core)
    up_ring = 1 + core * (RING - 2)

    barrier = pltpu.get_barrier_semaphore()
    peers = [partner, at_y(1), at_y(RING - 1)]
    peers += [at_x(step) for step in range(1, RING)] + [at_z(step) for step in range(1, RING)]
    for peer in peers:
        pl.semaphore_signal(barrier, inc=1, device_id=peer, device_id_type=MESH)

    def w_copy(index):
        offset = (index + 1) // 2
        dest = lax.rem(y + (4 - offset if index % 2 else 4 + offset), RING)
        return pltpu.make_async_copy(
            w_h.at[pl.ds(dest * 2 * width, 2 * width), :], w_v.at[index], w_sem.at[index]
        )

    loads = [
        pltpu.make_async_copy(src, dst, local_sem.at[n])
        for n, (src, dst) in enumerate(
            ((up_h, up_v), (dec_h, dec_v), (res_h, res_v), (skip_h, skip_v), (sig_h, sig_v))
        )
    ]
    loads[0].start()
    w_copy(0).start()
    w_copy(1).start()
    for load in loads[1:]:
        load.start()
    for index in range(2, RING):
        w_copy(index).start()

    def piece(part, peer):
        first, cols = (peer % per_half) * share, (peer // per_half) * lanes
        return part[first : first + share, cols : cols + lanes]

    def pair_copy(index):
        return pltpu.make_async_remote_copy(
            src_ref=pair_s.at[index], dst_ref=pair_r.at[index],
            send_sem=pair_ss.at[index], recv_sem=pair_rs.at[index],
            device_id=partner, device_id_type=MESH,
        )

    def product(index):
        w_copy(index).wait()
        for mine in (0, 1):
            side = lax.rem(core + 1 + mine, 2) * width
            part = lax.dot_general(
                up_v[...], w_v[index, pl.ds(pl.multiple_of(side, width), width), :],
                (((1,), (1,)), ((), ())), preferred_element_type=F32,
            )
            if mine:
                own[index] = part
            else:
                pair_s[index] = part.astype(BF16)
                if index > 0:
                    pair_copy(index).start()

    def ring_copy(far, send):
        slot = send if far else send + len(FAR_WAY)
        return pltpu.make_async_remote_copy(
            src_ref=ring_s.at[slot], dst_ref=ring_r.at[slot],
            send_sem=ring_ss.at[slot], recv_sem=ring_rs.at[slot],
            device_id=at_y(up_ring if far else RING - up_ring), device_id_type=MESH,
        )

    arrived = set()

    def chip_sum(far, dist, part):
        if dist == 0:
            index = RING - 1
        elif dist == per_half:
            index = 0
        else:
            index = 2 * (per_half - dist) + (core - 1 if far else -core)
        if (far, dist) not in arrived:
            arrived.add((far, dist))
            pair_copy(index).wait_recv()
        span = pl.ds(part * part_rows, part_rows)
        return own[index, span, :] + pair_r[index, span, :].astype(F32)

    def incoming_sum(far, send):
        ring_copy(far, send).wait_recv()
        return ring_r[send if far else send + len(FAR_WAY)].astype(F32)

    def ring_send(far, send):
        dist, part = (FAR_WAY if far else NEAR_WAY)[send]
        total = chip_sum(far, dist, part)
        if send >= PARTS:
            total = total + incoming_sum(far, send - PARTS)
        ring_s[send if far else send + len(FAR_WAY)] = total.astype(BF16)
        ring_copy(far, send).start()

    def x_copy(step, early):
        peer = lax.rem(x + step, RING)
        src, dst, ss, rs = (early_s, early_x, xe_ss, xe_rs) if early else (late_s, late_x, xl_ss, xl_rs)
        return pltpu.make_async_remote_copy(
            src_ref=src.at[peer], dst_ref=dst.at[x], send_sem=ss.at[step], recv_sem=rs.at[step],
            device_id=at_x(step), device_id_type=MESH,
        )

    def z_copy(step, early):
        ref, ss, rs = (early_z, ze_ss, ze_rs) if early else (late_z, zl_ss, zl_rs)
        return pltpu.make_async_remote_copy(
            src_ref=ref.at[z], dst_ref=ref.at[z], send_sem=ss.at[step], recv_sem=rs.at[step],
            device_id=at_z(step), device_id_type=MESH,
        )

    loads[0].wait()
    product(0)
    pl.semaphore_wait(barrier, len(peers))
    pair_copy(0).start()
    product(1)
    product(2)
    for send in range(PARTS):
        ring_send(True, send)
    product(3)
    product(4)
    for send in range(PARTS):
        ring_send(False, send)
    product(5)
    product(6)
    product(7)

    for load in loads[1:]:
        load.wait()
    pole = jnp.exp(dec_v[...] * (-1.0 / length))
    pole_block = jnp.exp(dec_v[...] * (-float(tokens) / length))
    gain = res_v[...] * (1.0 / length**0.5)
    small_o[pl.ds(modes, modes), :] = pole
    sig_f[...] = sig_v[...].astype(F32)
    zero = jnp.zeros((modes, width), F32)
    for peer in range(RING):
        jumps[peer, 0:share, :] = piece(pole_block, peer)

    def signal_steps(group, carry):
        state, slope = carry
        for step in range(8):
            row = sig_f[pl.ds(group * 8 + step, 1), :]
            state = (state + row) * pole
            slope = slope * pole + state
        return state, slope

    def signal_part(part, carry):
        groups = tokens // 8 // 4
        return lax.fori_loop(part * groups, (part + 1) * groups, signal_steps, carry)

    signal = signal_part(0, (zero, zero))
    for send in range(PARTS, 3 * PARTS):
        ring_send(True, send)
        ring_send(False, send)
        if send == PARTS + 1:
            signal = signal_part(1, signal)
        if send == 2 * PARTS - 1:
            signal = signal_part(2, signal)
        if send == 2 * PARTS + 1:
            signal = signal_part(3, signal)
            for peer in range(RING):
                early_s[peer] = jnp.concatenate([piece(signal[0], peer), piece(signal[1], peer)], axis=0)
            for step in PEER_ORDER:
                x_copy(step, True).start()
    early_x[x] = early_s[x]
    for send in range(3 * PARTS, 4 * PARTS):
        ring_send(True, send)

    def gradient_steps(last, group, carry):
        state, slope, res_sum, dec_sum = carry
        for step in range(8):
            pos = last - (group * 8 + step)
            grad = gc[pl.ds(pos, 1), :]
            row = sig_f[pl.ds(pos, 1), :]
            moved = state * pole
            state = grad + moved
            slope = slope * pole + moved
            res_sum = res_sum + row * state
            dec_sum = dec_sum + row * slope
            yl[pl.ds(pos, 1), :] = jnp.sum(gain * state, axis=0, keepdims=True)
        return state, slope, res_sum, dec_sum

    carry = (zero, zero, zero, zero)
    skip_sum = jnp.zeros((1, width), F32)
    for part in reversed(range(PARTS)):
        total = chip_sum(None, 0, part)
        for far, way in ((False, NEAR_WAY), (True, FAR_WAY)):
            total = total + incoming_sum(far, len(way) - 1 - part)
        total = total.astype(BF16).astype(F32)
        span = pl.ds(part * part_rows, part_rows)
        gc[span, :] = total
        skip_sum = skip_sum + jnp.sum(total * sig_f[span, :], axis=0, keepdims=True)
        carry = lax.fori_loop(
            0, part_rows // 8, functools.partial(gradient_steps, (part + 1) * part_rows - 1), carry
        )
    state, slope, res_sum, dec_sum = carry

    skip_rows = jnp.broadcast_to(skip_sum, (8, width))
    for peer in range(RING):
        cols = (peer // per_half) * lanes
        late_s[peer, 0:8, :] = jnp.concatenate([piece(state, peer), piece(slope, peer)], axis=0).astype(BF16)
        late_s[peer, 8:16, :] = jnp.concatenate([piece(res_sum, peer), piece(dec_sum, peer)], axis=0).astype(BF16)
        late_s[peer, 16:24, :] = skip_rows[:, cols : cols + lanes].astype(BF16)
    for step in PEER_ORDER:
        x_copy(step, False).start()
    late_x[x] = late_s[x]

    for step in range(1, RING):
        x_copy(step, True).wait_recv()
    jump = jumps[x, 0:share, :]
    empty = jnp.zeros((share, lanes), F32)
    sig_state, sig_slope = empty, empty
    for block in range(RING):
        sig_slope = early_x[block, share : 2 * share, :] + jump * (sig_slope + tokens * sig_state)
        sig_state = early_x[block, 0:share, :] + jump * sig_state
    early_z[z] = jnp.concatenate([sig_state, sig_slope], axis=0)
    for step in PEER_ORDER:
        z_copy(step, True).start()
    yl[...] = yl[...] + skip_v[...] * gc[...]
    base_copy = pltpu.make_async_copy(yl, base_o, local_sem.at[len(loads)])
    base_copy.start()
    for step in range(1, RING):
        x_copy(step, False).wait_recv()

    def parts_of(early, late, index):
        sums = late[index].astype(F32)
        early_part = early[index]
        return (
            sums[0:share], sums[share : 2 * share], sums[2 * share : 3 * share], sums[3 * share : 4 * share],
            sums[4 * share : 5 * share], early_part[0:share], early_part[share : 2 * share],
        )

    def join(parts, carry, jump, span):
        own_state, own_slope, own_res, own_dec, own_skip, sig_state, sig_slope = parts
        state, slope, res_sum, dec_sum, skip_sum = carry
        return (
            own_state + jump * state,
            own_slope + jump * (slope + span * state),
            res_sum + own_res + state * sig_state,
            dec_sum + own_dec + slope * sig_state + state * sig_slope,
            skip_sum + own_skip,
        )

    carry = (empty,) * 5
    for block in reversed(range(RING)):
        local_in[block] = carry[0]
        carry = join(parts_of(early_x, late_x, block), carry, jump, float(tokens))
    late_z[z, 0:8, :] = jnp.concatenate(carry[0:2], axis=0).astype(BF16)
    late_z[z, 8:16, :] = jnp.concatenate(carry[2:4], axis=0).astype(BF16)
    late_z[z, 16:24, :] = jnp.concatenate([carry[4], carry[4]], axis=0).astype(BF16)
    for step in PEER_ORDER:
        z_copy(step, False).start()
    row_jump = jump * jump
    row_jump = row_jump * row_jump
    row_jump = row_jump * row_jump
    for step in range(1, RING):
        z_copy(step, True).wait_recv()
    for step in range(1, RING):
        z_copy(step, False).wait_recv()

    incoming = empty
    carry = (empty,) * 5
    for row in reversed(range(RING)):
        incoming = jnp.where(z == row, carry[0], incoming)
        carry = join(parts_of(early_z, late_z, row), carry, row_jump, float(tokens * RING))
    for block in reversed(range(RING)):
        back[block, 0:8, :] = jnp.concatenate([local_in[block] + incoming, carry[2]], axis=0).astype(BF16)
        back[block, 8:16, :] = jnp.concatenate([carry[3], carry[4]], axis=0).astype(BF16)
        incoming = incoming * jump

    def b_copy(step):
        return pltpu.make_async_remote_copy(
            src_ref=back.at[lax.rem(x + step, RING)], dst_ref=full.at[x],
            send_sem=b_ss.at[step], recv_sem=b_rs.at[step],
            device_id=at_x(step), device_id_type=MESH,
        )

    for step in PEER_ORDER:
        b_copy(step).start()
    full[x] = back[x]
    base_copy.wait()
    for index in range(RING):
        pair_copy(index).wait_send()
    for far, way in ((True, FAR_WAY), (False, NEAR_WAY)):
        for send in range(len(way)):
            ring_copy(far, send).wait_send()
    for step in range(1, RING):
        for early in (True, False):
            x_copy(step, early).wait_send()
            z_copy(step, early).wait_send()
    for step in range(1, RING):
        b_copy(step).wait_recv()

    for peer in range(RING):
        cols = pl.ds((peer // per_half) * lanes, lanes)
        first = (peer % per_half) * share
        sums = full[peer].astype(F32)
        for line in range(3):
            small_o[pl.ds((0, 2, 3)[line] * modes + first, share), cols] = sums[line * share : (line + 1) * share]
        if peer % per_half == 0:
            small_o[pl.ds(4 * modes, 8), cols] = sums[2 * share : 4 * share]
    here = pl.ds(0, modes)
    small_o[here, :] = small_o[here, :] * gain
    here = pl.ds(2 * modes, modes)
    small_o[here, :] = small_o[here, :] * (1.0 / length)
    here = pl.ds(3 * modes, modes)
    small_o[here, :] = small_o[here, :] * (-1.0 / length) * (1.0 / length) * res_v[...]
    here = pl.ds(4 * modes, 8)
    small_o[here, :] = small_o[here, :] * (1.0 / length**0.5)
    for step in range(1, RING):
        b_copy(step).wait_send()


def finish(base, small, out, res_o, dec_o, skip_o, late):
    tokens = base.shape[0]
    modes = res_o.shape[0]
    res_o[...] = small[pl.ds(2 * modes, modes), :]
    dec_o[...] = small[pl.ds(3 * modes, modes), :]
    skip_o[...] = small[pl.ds(4 * modes + 4, 1), :]
    pole = small[pl.ds(modes, modes), :]

    def late_steps(group, term):
        for step in range(8):
            term = term * pole
            late[pl.ds(tokens - 1 - (group * 8 + step), 1), :] = jnp.sum(term, axis=0, keepdims=True)
        return term

    lax.fori_loop(0, tokens // 8, late_steps, small[pl.ds(0, modes), :])
    out[...] = (base[...] + late[...]).astype(BF16)


def body(signal, upstream, out_weight, residues, decays, skip_gain):
    tokens, width = signal.shape
    features = upstream.shape[1]
    modes = residues.shape[1]
    lanes = width // 2
    share = 2 * modes // RING
    in_hbm = pl.BlockSpec(memory_space=pltpu.HBM)
    any_ref = pl.BlockSpec(memory_space=pl.ANY)
    in_vmem = pl.BlockSpec(memory_space=pltpu.VMEM)
    dma = pltpu.SemaphoreType.DMA
    args = (signal, upstream, out_weight, residues.T, decays.T, skip_gain.reshape(1, width))
    base, small = pl.pallas_call(
        kernel,
        out_shape=(
            jax.ShapeDtypeStruct((tokens, width), F32),
            jax.ShapeDtypeStruct((4 * modes + 8, width), F32),
        ),
        in_specs=[in_hbm] * 6,
        out_specs=(any_ref, in_vmem),
        scratch_shapes=[
            pltpu.VMEM((tokens, width), BF16),
            pltpu.VMEM((tokens, features), BF16),
            pltpu.VMEM((RING, 2 * width, features), BF16),
            pltpu.VMEM((modes, width), F32),
            pltpu.VMEM((modes, width), F32),
            pltpu.VMEM((1, width), F32),
            pltpu.VMEM((tokens, width), F32),
            pltpu.VMEM((RING, tokens, width), BF16),
            pltpu.VMEM((RING, tokens, width), BF16),
            pltpu.VMEM((RING, tokens, width), F32),
            pltpu.VMEM((SENDS, tokens // PARTS, width), BF16),
            pltpu.VMEM((SENDS, tokens // PARTS, width), BF16),
            pltpu.VMEM((tokens, width), F32),
            pltpu.VMEM((tokens, width), F32),
            pltpu.VMEM((RING, 2 * share, lanes), F32),
            pltpu.VMEM((RING, 6 * share, lanes), BF16),
            pltpu.VMEM((RING, 2 * share, lanes), F32),
            pltpu.VMEM((RING, 6 * share, lanes), BF16),
            pltpu.VMEM((RING, 2 * share, lanes), F32),
            pltpu.VMEM((RING, 6 * share, lanes), BF16),
            pltpu.VMEM((RING, 2 * share, lanes), F32),
            pltpu.VMEM((RING, share, lanes), F32),
            pltpu.VMEM((RING, 4 * share, lanes), BF16),
            pltpu.VMEM((RING, 4 * share, lanes), BF16),
            dma((6,)), dma((RING,)), dma((RING,)), dma((RING,)), dma((SENDS,)), dma((SENDS,)),
        ] + [dma((RING,))] * 10,
        compiler_params=pltpu.CompilerParams(
            collective_id=0, has_side_effects=True, vmem_limit_bytes=24 << 20
        ),
    )(*(pltpu.with_memory_space_constraint(a, pltpu.HBM) for a in args))
    grad_signal, res_t, dec_t, skip = pl.pallas_call(
        finish,
        out_shape=(
            jax.ShapeDtypeStruct((tokens, width), BF16),
            jax.ShapeDtypeStruct((modes, width), F32),
            jax.ShapeDtypeStruct((modes, width), F32),
            jax.ShapeDtypeStruct((1, width), F32),
        ),
        in_specs=[in_vmem] * 2,
        out_specs=(in_vmem,) * 4,
        scratch_shapes=[pltpu.VMEM((tokens, width), F32)],
        compiler_params=pltpu.CompilerParams(vmem_limit_bytes=8 << 20),
    )(base, small)
    return grad_signal, res_t.T, dec_t.T, skip.reshape(width)


def solution(mesh):
    placed = (P("ctx", "ch"), P("ctx", "ch"), P(None, "ch"), P("ch", None), P("ch", None), P("ch"))
    return jax.shard_map(
        body,
        mesh=mesh,
        in_specs=placed,
        out_specs=(P("ctx", "ch"), P("ch", None), P("ch", None), P("ch")),
        check_vma=False,
    )
```

```python
import functools

import jax
import jax.numpy as jnp
from jax import lax
from jax.experimental import pallas as pl
from jax.experimental.pallas import tpu as pltpu
from jax.sharding import PartitionSpec as P

MESH = pl.DeviceIdType.MESH
F32 = jnp.float32
BF16 = jnp.bfloat16
RING = 8
PARTS = 4
PEER_ORDER = (4, 3, 5, 2, 6, 1, 7)
FAR_WAY = tuple((dist, part) for dist in (4, 3, 2, 1) for part in reversed(range(PARTS)))
NEAR_WAY = FAR_WAY[PARTS:]
SENDS = len(FAR_WAY) + len(NEAR_WAY)


def kernel(
    sig_h, up_h, w_h, res_h, dec_h, skip_h,
    base_o, small_o,
    sig_v, up_v, w_v, res_v, dec_v, skip_v,
    sig_f, pair_s, pair_r, own, ring_s, ring_r, gc, yl,
    early_s, late_s, early_x, late_x, early_z, late_z, jumps, local_in, back, full,
    local_sem, w_sem, pair_ss, pair_rs, ring_ss, ring_rs,
    xe_ss, xe_rs, xl_ss, xl_rs, ze_ss, ze_rs, zl_ss, zl_rs, b_ss, b_rs,
):
    tokens, width = sig_h.shape
    part_rows = tokens // PARTS
    lanes = width // 2
    modes = res_h.shape[0]
    share = 2 * modes // RING
    per_half = RING // 2
    length = tokens * RING * RING
    ctx = lax.axis_index("ctx")
    ch = lax.axis_index("ch")
    z, x = lax.div(ctx, RING), lax.rem(ctx, RING)
    y, core = lax.div(ch, 2), lax.rem(ch, 2)

    def at_x(step):
        return (z * RING + lax.rem(x + step, RING), ch)

    def at_z(step):
        return (lax.rem(z + step, RING) * RING + x, ch)

    def at_y(step):
        return (ctx, lax.rem(y + step, RING) * 2 + core)

    partner = (ctx, y * 2 + 1 - core)
    up_ring = 1 + core * (RING - 2)

    barrier = pltpu.get_barrier_semaphore()
    peers = [partner, at_y(1), at_y(RING - 1)]
    peers += [at_x(step) for step in range(1, RING)] + [at_z(step) for step in range(1, RING)]
    for peer in peers:
        pl.semaphore_signal(barrier, inc=1, device_id=peer, device_id_type=MESH)

    def w_copy(index):
        offset = (index + 1) // 2
        dest = lax.rem(y + (4 - offset if index % 2 else 4 + offset), RING)
        return pltpu.make_async_copy(
            w_h.at[pl.ds(dest * 2 * width, 2 * width), :], w_v.at[index], w_sem.at[index]
        )

    loads = [
        pltpu.make_async_copy(src, dst, local_sem.at[n])
        for n, (src, dst) in enumerate(
            ((up_h, up_v), (dec_h, dec_v), (res_h, res_v), (skip_h, skip_v), (sig_h, sig_v))
        )
    ]
    loads[0].start()
    w_copy(0).start()
    w_copy(1).start()
    for load in loads[1:]:
        load.start()
    for index in range(2, RING):
        w_copy(index).start()

    def piece(part, peer):
        first, cols = (peer % per_half) * share, (peer // per_half) * lanes
        return part[first : first + share, cols : cols + lanes]

    def pair_copy(index):
        return pltpu.make_async_remote_copy(
            src_ref=pair_s.at[index], dst_ref=pair_r.at[index],
            send_sem=pair_ss.at[index], recv_sem=pair_rs.at[index],
            device_id=partner, device_id_type=MESH,
        )

    def product(index):
        w_copy(index).wait()
        for mine in (0, 1):
            side = lax.rem(core + 1 + mine, 2) * width
            part = lax.dot_general(
                up_v[...], w_v[index, pl.ds(pl.multiple_of(side, width), width), :],
                (((1,), (1,)), ((), ())), preferred_element_type=F32,
            )
            if mine:
                own[index] = part
            else:
                pair_s[index] = part.astype(BF16)
                if index > 0:
                    pair_copy(index).start()

    def ring_copy(far, send):
        slot = send if far else send + len(FAR_WAY)
        return pltpu.make_async_remote_copy(
            src_ref=ring_s.at[slot], dst_ref=ring_r.at[slot],
            send_sem=ring_ss.at[slot], recv_sem=ring_rs.at[slot],
            device_id=at_y(up_ring if far else RING - up_ring), device_id_type=MESH,
        )

    arrived = set()

    def chip_sum(far, dist, part):
        if dist == 0:
            index = RING - 1
        elif dist == per_half:
            index = 0
        else:
            index = 2 * (per_half - dist) + (core - 1 if far else -core)
        if (far, dist) not in arrived:
            arrived.add((far, dist))
            pair_copy(index).wait_recv()
        span = pl.ds(part * part_rows, part_rows)
        return own[index, span, :] + pair_r[index, span, :].astype(F32)

    def incoming_sum(far, send):
        ring_copy(far, send).wait_recv()
        return ring_r[send if far else send + len(FAR_WAY)].astype(F32)

    def ring_send(far, send):
        dist, part = (FAR_WAY if far else NEAR_WAY)[send]
        total = chip_sum(far, dist, part)
        if send >= PARTS:
            total = total + incoming_sum(far, send - PARTS)
        ring_s[send if far else send + len(FAR_WAY)] = total.astype(BF16)
        ring_copy(far, send).start()

    def x_copy(step, early):
        peer = lax.rem(x + step, RING)
        src, dst, ss, rs = (early_s, early_x, xe_ss, xe_rs) if early else (late_s, late_x, xl_ss, xl_rs)
        return pltpu.make_async_remote_copy(
            src_ref=src.at[peer], dst_ref=dst.at[x], send_sem=ss.at[step], recv_sem=rs.at[step],
            device_id=at_x(step), device_id_type=MESH,
        )

    def z_copy(step, early):
        ref, ss, rs = (early_z, ze_ss, ze_rs) if early else (late_z, zl_ss, zl_rs)
        return pltpu.make_async_remote_copy(
            src_ref=ref.at[z], dst_ref=ref.at[z], send_sem=ss.at[step], recv_sem=rs.at[step],
            device_id=at_z(step), device_id_type=MESH,
        )

    loads[0].wait()
    product(0)
    pl.semaphore_wait(barrier, len(peers))
    pair_copy(0).start()
    product(1)
    product(2)
    for send in range(PARTS):
        ring_send(True, send)
    product(3)
    product(4)
    for send in range(PARTS):
        ring_send(False, send)
    product(5)
    product(6)
    product(7)

    for load in loads[1:]:
        load.wait()
    pole = jnp.exp(dec_v[...] * (-1.0 / length))
    pole_block = jnp.exp(dec_v[...] * (-float(tokens) / length))
    gain = res_v[...] * (1.0 / length**0.5)
    small_o[pl.ds(modes, modes), :] = pole
    sig_f[...] = sig_v[...].astype(F32)
    zero = jnp.zeros((modes, width), F32)
    for peer in range(RING):
        jumps[peer, 0:share, :] = piece(pole_block, peer)

    def signal_steps(group, carry):
        state, slope = carry
        for step in range(8):
            row = sig_f[pl.ds(group * 8 + step, 1), :]
            state = (state + row) * pole
            slope = slope * pole + state
        return state, slope

    def signal_part(part, carry):
        groups = tokens // 8 // 4
        return lax.fori_loop(part * groups, (part + 1) * groups, signal_steps, carry)

    signal = signal_part(0, (zero, zero))
    for send in range(PARTS, 3 * PARTS):
        ring_send(True, send)
        ring_send(False, send)
        if send == PARTS + 1:
            signal = signal_part(1, signal)
        if send == 2 * PARTS - 1:
            signal = signal_part(2, signal)
        if send == 2 * PARTS + 1:
            signal = signal_part(3, signal)
            for peer in range(RING):
                early_s[peer] = jnp.concatenate([piece(signal[0], peer), piece(signal[1], peer)], axis=0)
            for step in PEER_ORDER:
                x_copy(step, True).start()
    early_x[x] = early_s[x]
    for send in range(3 * PARTS, 4 * PARTS):
        ring_send(True, send)

    def gradient_steps(last, group, carry):
        state, slope, res_sum, dec_sum = carry
        for step in range(8):
            pos = last - (group * 8 + step)
            grad = gc[pl.ds(pos, 1), :]
            row = sig_f[pl.ds(pos, 1), :]
            moved = state * pole
            state = grad + moved
            slope = slope * pole + moved
            res_sum = res_sum + row * state
            dec_sum = dec_sum + row * slope
        return state, slope, res_sum, dec_sum

    carry = (zero, zero, zero, zero)
    skip_sum = jnp.zeros((1, width), F32)
    for part in reversed(range(PARTS)):
        total = chip_sum(None, 0, part)
        for far, way in ((False, NEAR_WAY), (True, FAR_WAY)):
            total = total + incoming_sum(far, len(way) - 1 - part)
        total = total.astype(BF16).astype(F32)
        span = pl.ds(part * part_rows, part_rows)
        gc[span, :] = total
        skip_sum = skip_sum + jnp.sum(total * sig_f[span, :], axis=0, keepdims=True)
        carry = lax.fori_loop(
            0, part_rows // 8, functools.partial(gradient_steps, (part + 1) * part_rows - 1), carry
        )
    state, slope, res_sum, dec_sum = carry

    skip_rows = jnp.broadcast_to(skip_sum, (8, width))
    for peer in range(RING):
        cols = (peer // per_half) * lanes
        late_s[peer, 0:8, :] = jnp.concatenate([piece(state, peer), piece(slope, peer)], axis=0).astype(BF16)
        late_s[peer, 8:16, :] = jnp.concatenate([piece(res_sum, peer), piece(dec_sum, peer)], axis=0).astype(BF16)
        late_s[peer, 16:24, :] = skip_rows[:, cols : cols + lanes].astype(BF16)
    for step in PEER_ORDER:
        x_copy(step, False).start()
    late_x[x] = late_s[x]

    for step in range(1, RING):
        x_copy(step, True).wait_recv()
    jump = jumps[x, 0:share, :]
    empty = jnp.zeros((share, lanes), F32)
    sig_state, sig_slope = empty, empty
    for block in range(RING):
        sig_slope = early_x[block, share : 2 * share, :] + jump * (sig_slope + tokens * sig_state)
        sig_state = early_x[block, 0:share, :] + jump * sig_state
    early_z[z] = jnp.concatenate([sig_state, sig_slope], axis=0)
    for step in PEER_ORDER:
        z_copy(step, True).start()

    def local_steps(group, state):
        for step in range(8):
            pos = tokens - 1 - (group * 8 + step)
            state = gc[pl.ds(pos, 1), :] + state * pole
            yl[pl.ds(pos, 1), :] = jnp.sum(gain * state, axis=0, keepdims=True)
        return state

    lax.fori_loop(0, tokens // 8, local_steps, zero)
    yl[...] = yl[...] + skip_v[...] * gc[...]
    base_copy = pltpu.make_async_copy(yl, base_o, local_sem.at[len(loads)])
    base_copy.start()
    for step in range(1, RING):
        x_copy(step, False).wait_recv()

    def parts_of(early, late, index):
        sums = late[index].astype(F32)
        early_part = early[index]
        return (
            sums[0:share], sums[share : 2 * share], sums[2 * share : 3 * share], sums[3 * share : 4 * share],
            sums[4 * share : 5 * share], early_part[0:share], early_part[share : 2 * share],
        )

    def join(parts, carry, jump, span):
        own_state, own_slope, own_res, own_dec, own_skip, sig_state, sig_slope = parts
        state, slope, res_sum, dec_sum, skip_sum = carry
        return (
            own_state + jump * state,
            own_slope + jump * (slope + span * state),
            res_sum + own_res + state * sig_state,
            dec_sum + own_dec + slope * sig_state + state * sig_slope,
            skip_sum + own_skip,
        )

    carry = (empty,) * 5
    for block in reversed(range(RING)):
        local_in[block] = carry[0]
        carry = join(parts_of(early_x, late_x, block), carry, jump, float(tokens))
    late_z[z, 0:8, :] = jnp.concatenate(carry[0:2], axis=0).astype(BF16)
    late_z[z, 8:16, :] = jnp.concatenate(carry[2:4], axis=0).astype(BF16)
    late_z[z, 16:24, :] = jnp.concatenate([carry[4], carry[4]], axis=0).astype(BF16)
    for step in PEER_ORDER:
        z_copy(step, False).start()
    row_jump = jump * jump
    row_jump = row_jump * row_jump
    row_jump = row_jump * row_jump
    for step in range(1, RING):
        z_copy(step, True).wait_recv()
    for step in range(1, RING):
        z_copy(step, False).wait_recv()

    incoming = empty
    carry = (empty,) * 5
    for row in reversed(range(RING)):
        incoming = jnp.where(z == row, carry[0], incoming)
        carry = join(parts_of(early_z, late_z, row), carry, row_jump, float(tokens * RING))
    for block in reversed(range(RING)):
        back[block, 0:8, :] = jnp.concatenate([local_in[block] + incoming, carry[2]], axis=0).astype(BF16)
        back[block, 8:16, :] = jnp.concatenate([carry[3], carry[4]], axis=0).astype(BF16)
        incoming = incoming * jump

    def b_copy(step):
        return pltpu.make_async_remote_copy(
            src_ref=back.at[lax.rem(x + step, RING)], dst_ref=full.at[x],
            send_sem=b_ss.at[step], recv_sem=b_rs.at[step],
            device_id=at_x(step), device_id_type=MESH,
        )

    for step in PEER_ORDER:
        b_copy(step).start()
    full[x] = back[x]
    base_copy.wait()
    for index in range(RING):
        pair_copy(index).wait_send()
    for far, way in ((True, FAR_WAY), (False, NEAR_WAY)):
        for send in range(len(way)):
            ring_copy(far, send).wait_send()
    for step in range(1, RING):
        for early in (True, False):
            x_copy(step, early).wait_send()
            z_copy(step, early).wait_send()
    for step in range(1, RING):
        b_copy(step).wait_recv()

    for peer in range(RING):
        cols = pl.ds((peer // per_half) * lanes, lanes)
        first = (peer % per_half) * share
        sums = full[peer].astype(F32)
        for line in range(3):
            small_o[pl.ds((0, 2, 3)[line] * modes + first, share), cols] = sums[line * share : (line + 1) * share]
        if peer % per_half == 0:
            small_o[pl.ds(4 * modes, 8), cols] = sums[2 * share : 4 * share]
    here = pl.ds(0, modes)
    small_o[here, :] = small_o[here, :] * gain
    here = pl.ds(2 * modes, modes)
    small_o[here, :] = small_o[here, :] * (1.0 / length)
    here = pl.ds(3 * modes, modes)
    small_o[here, :] = small_o[here, :] * (-1.0 / length) * (1.0 / length) * res_v[...]
    here = pl.ds(4 * modes, 8)
    small_o[here, :] = small_o[here, :] * (1.0 / length**0.5)
    for step in range(1, RING):
        b_copy(step).wait_send()


def finish(base, small, out, res_o, dec_o, skip_o, late):
    tokens = base.shape[0]
    modes = res_o.shape[0]
    res_o[...] = small[pl.ds(2 * modes, modes), :]
    dec_o[...] = small[pl.ds(3 * modes, modes), :]
    skip_o[...] = small[pl.ds(4 * modes + 4, 1), :]
    pole = small[pl.ds(modes, modes), :]

    def late_steps(group, term):
        for step in range(8):
            term = term * pole
            late[pl.ds(tokens - 1 - (group * 8 + step), 1), :] = jnp.sum(term, axis=0, keepdims=True)
        return term

    lax.fori_loop(0, tokens // 8, late_steps, small[pl.ds(0, modes), :])
    out[...] = (base[...] + late[...]).astype(BF16)


def body(signal, upstream, out_weight, residues, decays, skip_gain):
    tokens, width = signal.shape
    features = upstream.shape[1]
    modes = residues.shape[1]
    lanes = width // 2
    share = 2 * modes // RING
    in_hbm = pl.BlockSpec(memory_space=pltpu.HBM)
    any_ref = pl.BlockSpec(memory_space=pl.ANY)
    in_vmem = pl.BlockSpec(memory_space=pltpu.VMEM)
    dma = pltpu.SemaphoreType.DMA
    args = (signal, upstream, out_weight, residues.T, decays.T, skip_gain.reshape(1, width))
    base, small = pl.pallas_call(
        kernel,
        out_shape=(
            jax.ShapeDtypeStruct((tokens, width), F32),
            jax.ShapeDtypeStruct((4 * modes + 8, width), F32),
        ),
        in_specs=[in_hbm] * 6,
        out_specs=(any_ref, in_vmem),
        scratch_shapes=[
            pltpu.VMEM((tokens, width), BF16),
            pltpu.VMEM((tokens, features), BF16),
            pltpu.VMEM((RING, 2 * width, features), BF16),
            pltpu.VMEM((modes, width), F32),
            pltpu.VMEM((modes, width), F32),
            pltpu.VMEM((1, width), F32),
            pltpu.VMEM((tokens, width), F32),
            pltpu.VMEM((RING, tokens, width), BF16),
            pltpu.VMEM((RING, tokens, width), BF16),
            pltpu.VMEM((RING, tokens, width), F32),
            pltpu.VMEM((SENDS, tokens // PARTS, width), BF16),
            pltpu.VMEM((SENDS, tokens // PARTS, width), BF16),
            pltpu.VMEM((tokens, width), F32),
            pltpu.VMEM((tokens, width), F32),
            pltpu.VMEM((RING, 2 * share, lanes), F32),
            pltpu.VMEM((RING, 6 * share, lanes), BF16),
            pltpu.VMEM((RING, 2 * share, lanes), F32),
            pltpu.VMEM((RING, 6 * share, lanes), BF16),
            pltpu.VMEM((RING, 2 * share, lanes), F32),
            pltpu.VMEM((RING, 6 * share, lanes), BF16),
            pltpu.VMEM((RING, 2 * share, lanes), F32),
            pltpu.VMEM((RING, share, lanes), F32),
            pltpu.VMEM((RING, 4 * share, lanes), BF16),
            pltpu.VMEM((RING, 4 * share, lanes), BF16),
            dma((6,)), dma((RING,)), dma((RING,)), dma((RING,)), dma((SENDS,)), dma((SENDS,)),
        ] + [dma((RING,))] * 10,
        compiler_params=pltpu.CompilerParams(
            collective_id=0, has_side_effects=True, vmem_limit_bytes=24 << 20
        ),
    )(*(pltpu.with_memory_space_constraint(a, pltpu.HBM) for a in args))
    grad_signal, res_t, dec_t, skip = pl.pallas_call(
        finish,
        out_shape=(
            jax.ShapeDtypeStruct((tokens, width), BF16),
            jax.ShapeDtypeStruct((modes, width), F32),
            jax.ShapeDtypeStruct((modes, width), F32),
            jax.ShapeDtypeStruct((1, width), F32),
        ),
        in_specs=[in_vmem] * 2,
        out_specs=(in_vmem,) * 4,
        scratch_shapes=[pltpu.VMEM((tokens, width), F32)],
        compiler_params=pltpu.CompilerParams(vmem_limit_bytes=8 << 20),
    )(base, small)
    return grad_signal, res_t.T, dec_t.T, skip.reshape(width)


def solution(mesh):
    placed = (P("ctx", "ch"), P("ctx", "ch"), P(None, "ch"), P("ch", None), P("ch", None), P("ch"))
    return jax.shard_map(
        body,
        mesh=mesh,
        in_specs=placed,
        out_specs=(P("ctx", "ch"), P("ch", None), P("ch", None), P("ch")),
        check_vma=False,
    )
```
